256 devices in a mesh: dp: 32 (over x, z), seq: 8 (over y, core).
Axes of the slice: x: 4, y: 4, z: 8, core: 2. Of those that a mesh axis runs over, the one named last changes fastest.
Arguments:
- span_store: bfloat16 [32, 512, 8192], P('dp', 'seq'), may hold values from -6 to 6
- target: int32 [32, 512], P('dp', 'seq'), may hold values from 0 to 31, as said below
- segment_ids: int32 [32, 512], P('dp'), may hold values from 0 to 7, never falling along the last dimension, each value on 1 to 128 neighbouring positions
- norm_gain: float32 [8192], replicated, may hold values from 0.25 to 1.75
- w_query: bfloat16 [8192, 4096], P('dp', 'seq'), may hold values from -0.0625 to 0.0625
- key_weight: bfloat16 [8192, 1024], P('dp', 'seq'), may hold values from -0.0625 to 0.0625
- value_weight: bfloat16 [8192, 1024], P('dp', 'seq'), may hold values from -0.0625 to 0.0625
Outputs:
- context: bfloat16 [32, 512, 4096], P('dp', 'seq')
The draws below stay inside these ranges and needn't reach their ends.
Inputs may be any that keep to these rules, and one draw needn't show every extreme that they name: `target`: within one lane, the stored tokens of all shards that name one packed row number exactly 64; one shard's tokens of one lane name one row at most 3 times, and exactly 3 times for some shard and row in every lane. `segment_ids`: along a row, document ids never fall.
All inputs are finite; a program needn't handle non-finite values.
Results may differ from the reference program's by a relative error of at most 0.0079.
Values may be sent and summed in bfloat16 or wider, within the bound.
No kernel may reach another device: no remote copies, remote signals or barrier semaphores. Data moves between devices by JAX's collectives and lax.ppermute only.
A program may use at most 128 MiB of HBM per device.

```python
import math
import jax
import jax.numpy as jnp
import numpy as np
from jax import lax

MODEL_WIDTH = 8192
QUERY_HEADS = 32
KEY_VALUE_HEADS = 8
HEAD_SIZE = 128
TOK_DEV = 64
PACKED_LENGTH = 512
ROWS = 32
N_DP = 32
N_SEQ = 8


def draw_target(key, part):
    average = TOK_DEV // N_DP
    step_size = average // 2

    def one_lane(lane_key):
        perm_key, shift_key, order_key, shuffle_key, coin_key = jax.random.split(lane_key, 5)
        sigma = jax.random.permutation(perm_key, N_DP).astype(jnp.int32)
        offset = jax.random.randint(shift_key, (), 1, N_DP).astype(jnp.int32)
        tau = (sigma + offset) % N_DP
        columns = jnp.arange(N_DP, dtype=jnp.int32)
        plus_part = (columns[None, :] == sigma[:, None]).astype(jnp.int32)
        minus_part = (columns[None, :] == tau[:, None]).astype(jnp.int32)
        counts = average + step_size * plus_part - step_size * minus_part
        row_orders = jax.vmap(lambda one_key: jax.random.permutation(one_key, N_DP).astype(jnp.int32))(jax.random.split(order_key, N_DP))
        ordered_counts = jnp.take_along_axis(counts, row_orders, axis=1)
        span_ends = jnp.cumsum(ordered_counts, axis=1)
        slot_ids = jnp.arange(TOK_DEV, dtype=jnp.int32)
        span_ids = jnp.sum((span_ends[:, None, :] <= slot_ids[None, :, None]).astype(jnp.int32), axis=2)
        contiguous = jnp.take_along_axis(row_orders, span_ids, axis=1)
        shuffles = jax.vmap(lambda one_key: jax.random.permutation(one_key, TOK_DEV).astype(jnp.int32))(jax.random.split(shuffle_key, N_DP))
        shuffled = jnp.take_along_axis(contiguous, shuffles, axis=1)
        coins = jax.random.randint(coin_key, (N_DP, 1), 0, 2).astype(jnp.int32)
        return jnp.where(coins == 1, shuffled, contiguous)
    lane_keys = jax.random.split(jax.random.fold_in(key, 11), N_SEQ)
    per_lane = jax.vmap(one_lane)(lane_keys)
    return jnp.transpose(per_lane, (1, 0, 2)).reshape(N_DP, N_SEQ * TOK_DEV).astype(jnp.int32)


def block_scale(own_key, shape, pieces, low, high):
    level, own = 1.0, jax.random.fold_in(own_key, 6)
    for dim, parts in pieces:
        heights = jnp.exp(jax.random.uniform(jax.random.fold_in(own, dim), (parts,), jnp.float32, low / len(pieces), high / len(pieces)))
        level = level * jnp.repeat(heights, shape[dim] // parts).reshape([-1 if axis == dim else 1 for axis in range(len(shape))])
    return level


def split_up(amount, total, limit, lean):
    loads = [(1 << 20) // math.isqrt(grade ** lean) + 1 for grade in range(2, amount + 1)]
    rest, given = total - limit - (amount - 1), [1] * (amount - 1)
    while rest > 0:
        free = [i for i in range(amount - 1) if given[i] < limit]
        pool, left = sum([loads[i] for i in free]), rest
        for i in free:
            addition = min(limit - given[i], max(1, left * loads[i] // pool), rest)
            given[i] = given[i] + addition
            rest = rest - addition
    return np.array([limit] + given)


def ragged(key, number_of, total, reach, lean):
    if number_of == 2:
        one = jax.random.randint(key, (), max(1, total - reach), min(reach, total - 1) + 1)
        return jnp.stack([one, total - one])
    sizes = jnp.asarray(split_up(number_of, total, reach, lean), jnp.int32)
    couples = (number_of - 1) // 2
    source_of, sink = sizes[1:1 + 2 * couples:2], sizes[2:2 + 2 * couples:2]
    margin = jnp.minimum(source_of - 1, reach - sink)
    passed = jax.random.randint(jax.random.fold_in(key, 1), (couples,), 0, 1 << 20) % (margin + 1)
    sizes = sizes.at[1:1 + 2 * couples:2].set(source_of - passed).at[2:2 + 2 * couples:2].set(sink + passed)
    return sizes[jax.random.permutation(jax.random.fold_in(key, 2), number_of)]


def scatter_about(own_key, extent, spread, limit, shards=(), held_as=jnp.bfloat16):
    level = block_scale(own_key, extent, shards, -0.22, 0.18) if shards else 1.0
    array = jax.random.normal(own_key, extent, jnp.float32) * spread * level
    return jnp.minimum(jnp.maximum(array, -limit), limit).astype(held_as)


def setup_inputs(seed: int = 0) -> dict:
    key_of = jax.random.split(jax.random.key(seed), 8)
    return {
        "span_store": scatter_about(key_of[0], (ROWS, PACKED_LENGTH, MODEL_WIDTH), 1.0, 6.0, ((0, 32), (1, 8))),
        "target": draw_target(jax.random.fold_in(key_of[7], 71), 0),
        "segment_ids": jax.vmap(lambda own: jnp.searchsorted(jnp.cumsum(ragged(own, max(PACKED_LENGTH // 64, 4), PACKED_LENGTH, PACKED_LENGTH // 4, 2)), jnp.arange(PACKED_LENGTH), side="right"))(jax.random.split(key_of[2], ROWS)).reshape((ROWS, PACKED_LENGTH)).astype(jnp.int32),
        "norm_gain": jnp.clip(1.0 + 0.15 * jax.random.normal(key_of[3], (MODEL_WIDTH,), jnp.float32), 0.25, 1.75),
        "w_query": scatter_about(key_of[4], (MODEL_WIDTH, QUERY_HEADS * HEAD_SIZE), MODEL_WIDTH ** -0.5, 0.0625, ((0, 32), (1, 8))),
        "key_weight": scatter_about(key_of[5], (MODEL_WIDTH, KEY_VALUE_HEADS * HEAD_SIZE), MODEL_WIDTH ** -0.5, 0.0625, ((0, 32), (1, 8))),
        "value_weight": scatter_about(key_of[6], (MODEL_WIDTH, KEY_VALUE_HEADS * HEAD_SIZE), MODEL_WIDTH ** -0.5, 0.0625, ((0, 32), (1, 8))),
    }


epsilon = 1e-05
rope_base = 500000.0

def rotary_angles(values, token_positions):
    half_dim = values.shape[-1] // 2
    exponent = jnp.arange(half_dim, dtype=jnp.float32) * (2.0 / values.shape[-1])
    frequency = rope_base ** (-exponent)
    angles = token_positions.astype(jnp.float32)[:, None] * frequency[None, :]
    cosine = jnp.concatenate([jnp.cos(angles), jnp.cos(angles)], axis=-1)[:, None, :]
    sine_part = jnp.concatenate([jnp.sin(angles), jnp.sin(angles)], axis=-1)[:, None, :]
    rotated = jnp.concatenate([-values[..., half_dim:], values[..., :half_dim]], axis=-1)
    return values * cosine + rotated * sine_part

def place_rows(span_store, target):
    packed = jnp.zeros((ROWS, PACKED_LENGTH, MODEL_WIDTH), jnp.bfloat16)
    owner_ids = jnp.arange(ROWS, dtype=jnp.int32)
    for lane_idx in range(N_SEQ):
        lane_start = lane_idx * TOK_DEV
        owners = target[:, lane_start:lane_start + TOK_DEV].reshape(-1)
        onehot = (owners[:, None] == owner_ids[None, :]).astype(jnp.int32)
        ranking = jnp.cumsum(onehot, axis=0) - onehot
        slot_index = lax.optimization_barrier(jnp.sum(ranking * onehot, axis=1)).astype(jnp.int32)
        sources = span_store[:, lane_start:lane_start + TOK_DEV, :].reshape(-1, MODEL_WIDTH)
        packed = packed.at[owners, slot_index + lane_start].set(sources)
    return packed

def reference(span_store, target, segment_ids, norm_gain, w_query, key_weight, value_weight):
    packed = place_rows(span_store, target)
    token_positions = jnp.arange(PACKED_LENGTH, dtype=jnp.int32)
    scaling = HEAD_SIZE ** (-0.5)

    def one_row(inputs):
        row_tokens, row_segments = inputs
        values = row_tokens.astype(jnp.float32)
        inverse = lax.rsqrt(lax.optimization_barrier(jnp.mean(values * values, axis=-1, keepdims=True)) + epsilon)
        input_normed = (values * inverse * norm_gain).astype(jnp.bfloat16)
        query_rows = rotary_angles(jnp.dot(input_normed, w_query, preferred_element_type=jnp.float32).reshape(PACKED_LENGTH, QUERY_HEADS, HEAD_SIZE), token_positions).astype(jnp.bfloat16)
        key_matrix = rotary_angles(jnp.dot(input_normed, key_weight, preferred_element_type=jnp.float32).reshape(PACKED_LENGTH, KEY_VALUE_HEADS, HEAD_SIZE), token_positions).astype(jnp.bfloat16)
        value_matrix = jnp.dot(input_normed, value_weight, preferred_element_type=jnp.float32).astype(jnp.bfloat16).reshape(PACKED_LENGTH, KEY_VALUE_HEADS, HEAD_SIZE)
        grouped_query = query_rows.reshape(PACKED_LENGTH, KEY_VALUE_HEADS, QUERY_HEADS // KEY_VALUE_HEADS, HEAD_SIZE)
        scores = jnp.einsum('qgrd,kgd->grqk', grouped_query.astype(jnp.float32), key_matrix.astype(jnp.float32)) * scaling
        allowed = (row_segments[:, None] == row_segments[None, :]) & (token_positions[None, :] <= token_positions[:, None])
        exp_terms = jnp.where(allowed, jnp.exp(scores), 0.0)
        weights = (exp_terms / lax.optimization_barrier(jnp.sum(exp_terms, axis=-1, keepdims=True))).astype(jnp.bfloat16)
        context = jnp.einsum('grqk,kgd->qgrd', weights.astype(jnp.float32), value_matrix.astype(jnp.float32))
        return context.astype(jnp.bfloat16).reshape(PACKED_LENGTH, QUERY_HEADS * HEAD_SIZE)
    return lax.map(one_row, (packed, segment_ids))
```

```python
import jax
import jax.numpy as jnp
from jax import lax
from jax.experimental import pallas as pl
from jax.experimental.pallas import tpu as pltpu
from jax.sharding import PartitionSpec as P

HEAD = 128
EPS = 1e-05
ROPE_BASE = 500000.0
NX, NZ = 4, 8
ND = NX * NZ
LANES = 8
LANE = 64
CAP = 3
SLOTS = LANES * CAP
KB = 256
EMPTY = 2.0**100
SELF = 128
DZ = (0, 1, 7, 2, 6, 3, 5, 4)


def from_z(value, k):
    pairs = [(x * NZ + (z + k) % NZ, x * NZ + z) for x in range(NX) for z in range(NZ)]
    return lax.ppermute(value, "dp", pairs)


def from_x(value, k):
    pairs = [(((x + k) % NX) * NZ + z, x * NZ + z) for x in range(NX) for z in range(NZ)]
    return lax.ppermute(value, "dp", pairs)


def normalize_kernel(order_ref, x_ref, gain_ref, out_ref):
    values = x_ref[...].astype(jnp.float32)
    inverse = lax.rsqrt(jnp.mean(values * values, axis=-1, keepdims=True) + EPS)
    for b in range(ND):
        start = pl.multiple_of(order_ref[b] * KB, KB)
        piece = x_ref[:, pl.ds(start, KB)].astype(jnp.float32)
        gain = gain_ref[:, pl.ds(start, KB)]
        out_ref[:, b * KB : (b + 1) * KB] = (piece * inverse * gain).astype(jnp.bfloat16)


def normalize(stored, norm_gain, order):
    vmem = pl.BlockSpec(memory_space=pltpu.VMEM)
    return pl.pallas_call(
        normalize_kernel,
        out_shape=jax.ShapeDtypeStruct(stored.shape, jnp.bfloat16),
        in_specs=[pl.BlockSpec(memory_space=pltpu.SMEM), vmem, vmem],
        out_specs=vmem,
    )(order, stored, norm_gain[None, :])


def attention_kernel(arr_ref, ahead_ref, segq_ref, segk_ref, cos_ref, sin_ref, out_ref):
    length = out_ref.shape[0]
    arrived = arr_ref.shape[0]
    valid = (arr_ref[:, :HEAD].astype(jnp.float32) < EMPTY / 2).astype(jnp.bfloat16)
    found = lax.dot_general(
        valid, ahead_ref[...], (((0,), (0,)), ((), ())), preferred_element_type=jnp.float32
    )[:1].astype(jnp.int32)
    lane = (lax.broadcasted_iota(jnp.int32, (1, arrived), 1) % SLOTS) // CAP
    place = jnp.where(found >= SELF, lane * LANE + found - SELF, -1)
    rows = lax.broadcasted_iota(jnp.int32, (length, arrived), 0)
    pick = (rows == place).astype(jnp.bfloat16)
    packed = jnp.dot(pick, arr_ref[...], preferred_element_type=jnp.float32)
    cosine, sine = cos_ref[...], sin_ref[...]

    def turn(u):
        return (u * cosine + pltpu.roll(u, HEAD // 2, 1) * sine).astype(jnp.bfloat16)

    heads = [turn(packed[:, h * HEAD : (h + 1) * HEAD]) for h in range(4)]
    key = turn(packed[:, 4 * HEAD : 5 * HEAD])
    value = packed[:, 5 * HEAD : 6 * HEAD].astype(jnp.bfloat16)
    block = 128
    for b in range(length // block):
        lo = max(b - 1, 0) * block
        hi = (b + 1) * block
        width = hi - lo
        keys, values = key[lo:hi], value[lo:hi]
        tpos = b * block + lax.broadcasted_iota(jnp.int32, (block, width), 0)
        upos = lo + lax.broadcasted_iota(jnp.int32, (block, width), 1)
        allowed = (segq_ref[b * block : hi, :] == segk_ref[:, lo:hi]) & (upos <= tpos)
        for h in range(4):
            q = heads[h][b * block : hi]
            score = lax.dot_general(q, keys, (((1,), (1,)), ((), ())), preferred_element_type=jnp.float32)
            terms = jnp.where(allowed, jnp.exp(score * (HEAD ** -0.5)), 0.0)
            total = jnp.sum(terms, axis=-1, keepdims=True)
            weights = (terms / total).astype(jnp.bfloat16)
            context = jnp.dot(weights, values, preferred_element_type=jnp.float32)
            out_ref[b * block : hi, h * HEAD : (h + 1) * HEAD] = context.astype(jnp.bfloat16)


def attention(arrived, seg, cosine, sine):
    length = seg.shape[0]
    count = arrived.shape[0]
    col = jnp.arange(count, dtype=jnp.int32)
    lane = (col % SLOTS) // CAP
    ahead = ((lane[:, None] == lane[None, :]) & (col[:, None] < col[None, :])).astype(jnp.bfloat16)
    ahead = jnp.where(col[:, None] == col[None, :], float(SELF), ahead).astype(jnp.bfloat16)
    vmem = pl.BlockSpec(memory_space=pltpu.VMEM)
    return pl.pallas_call(
        attention_kernel,
        out_shape=jax.ShapeDtypeStruct((length, 4 * HEAD), jnp.bfloat16),
        in_specs=[vmem] * 6,
        out_specs=vmem,
        compiler_params=pltpu.CompilerParams(vmem_limit_bytes=32 << 20),
    )(arrived, ahead, seg[:, None], seg[None, :], cosine, sine)


def kv_kernel(n, tok_ref, *refs):
    out_ref = refs[-1]
    total = jnp.zeros(out_ref.shape, jnp.float32)
    for dz, ref in enumerate(refs[:-1]):
        for dx in range(NX):
            at = (dx * NZ + dz) * KB
            total += jnp.dot(
                tok_ref[:, at : at + KB], ref[dx * KB : (dx + 1) * KB, :], preferred_element_type=jnp.float32
            )
    out_ref[...] = total


def kv_part(tokens, blocks):
    vmem = pl.BlockSpec(memory_space=pltpu.VMEM)
    return pl.pallas_call(
        lambda *refs: kv_kernel(len(blocks), *refs),
        out_shape=jax.ShapeDtypeStruct((tokens.shape[0], blocks[0].shape[1]), jnp.float32),
        in_specs=[vmem] * (1 + len(blocks)),
        out_specs=vmem,
        compiler_params=pltpu.CompilerParams(vmem_limit_bytes=32 << 20),
    )(tokens, *blocks)


def dispatch_kernel(q_ref, kv_ref, slot_ref, out_ref):
    count, tokens = out_ref.shape[0], q_ref.shape[0]
    rows = lax.broadcasted_iota(jnp.int32, (count, tokens), 0)
    send = (rows == slot_ref[...]).astype(jnp.bfloat16)
    used = jnp.dot(send, jnp.ones((tokens, HEAD), jnp.bfloat16), preferred_element_type=jnp.float32) > 0.5
    for ref, at in ((q_ref, 0), (kv_ref, q_ref.shape[1])):
        moved = jnp.dot(send, ref[...].astype(jnp.bfloat16), preferred_element_type=jnp.float32)
        for c in range(0, ref.shape[1], HEAD):
            out_ref[:, at + c : at + c + HEAD] = jnp.where(used, moved[:, c : c + HEAD], EMPTY).astype(jnp.bfloat16)


def dispatch(q_acc, kv_acc, slot):
    vmem = pl.BlockSpec(memory_space=pltpu.VMEM)
    return pl.pallas_call(
        dispatch_kernel,
        out_shape=jax.ShapeDtypeStruct((ND * SLOTS, q_acc.shape[1] + kv_acc.shape[1]), jnp.bfloat16),
        in_specs=[vmem] * 3,
        out_specs=vmem,
        compiler_params=pltpu.CompilerParams(vmem_limit_bytes=32 << 20),
    )(q_acc, kv_acc, slot[None, :])


def rotary_tables(length):
    half = HEAD // 2
    frequency = ROPE_BASE ** (-(jnp.arange(half, dtype=jnp.float32) * (2.0 / HEAD)))
    angles = jnp.arange(length, dtype=jnp.float32)[:, None] * frequency[None, :]
    c, s = jnp.cos(angles), jnp.sin(angles)
    return jnp.concatenate([c, c], axis=-1), jnp.concatenate([-s, s], axis=-1)


def after(values, *done):
    return lax.optimization_barrier((values, done))[0]


def gather_weights(query, key_value):
    h = KB // 2
    xp, xm = from_x(key_value, 1), from_x(key_value, -1)
    zp, zm = [query, from_z(query, 1)], [query, from_z(query, -1)]
    xp_in, xm_in = after((xp[:h], xm[h:]), xp, xm)
    row = jnp.concatenate([key_value, xp, from_x(xp_in, 1), from_x(xm_in, -1), xm], axis=0)
    near = jnp.concatenate([query, zp[1], zm[1]], axis=0)
    n1, n3 = from_x(after(near, row), 1), from_x(after(near, row), -1)
    for _ in range(2):
        a, b = after((zp[-1], zm[-1]), zp[-1], zm[-1])
        zp.append(from_z(a, 1))
        zm.append(from_z(b, -1))
    a, b = after((zp[3][:h], zm[3][h:]), zp[3], zm[3])
    far = [zp[2], zm[2], zp[3], zm[3], from_z(a, 1), from_z(b, -1)]
    far = jnp.concatenate(far, axis=0)
    far_in = after(far, n1, n3)
    f1, f3 = from_x(far_in, 1), from_x(far_in, -1)
    g = near.shape[0] // 2
    a, b = after((n1[:g], n3[g:]), f1, f3)
    n2 = [from_x(a, 1), from_x(b, -1)]
    g = far.shape[0] // 2
    a, b = after((f1[:g], f3[g:]), *n2)
    f2 = [from_x(a, 1), from_x(b, -1)]
    rows_p, rows_m = [after(row, far)], [after(row, far)]
    for _ in range(3):
        a, b = after((rows_p[-1], rows_m[-1]), rows_p[-1], rows_m[-1])
        rows_p.append(from_z(a, 1))
        rows_m.append(from_z(b, -1))
    g = row.shape[0] // 2
    a, b = after((rows_p[3][:g], rows_m[3][g:]), rows_p[3], rows_m[3])
    last = jnp.concatenate([from_z(a, 1), from_z(b, -1)], axis=0)
    rows = [row, rows_p[1], rows_m[1], rows_p[2], rows_m[2], rows_p[3], rows_m[3], last]
    w = near.shape[0]
    columns = [(0, near), (w, far), (8 * KB, n1), (8 * KB + w, f1), (24 * KB, n3), (24 * KB + w, f3)]
    columns += [(16 * KB, n2[0]), (16 * KB + w // 2, n2[1])]
    columns += [(16 * KB + w, f2[0]), (16 * KB + w + far.shape[0] // 2, f2[1])]
    return columns, rows


def shards(span_store, target, segment_ids, norm_gain, w_query, key_weight, value_weight):
    dp = lax.axis_index("dp")
    seq = lax.axis_index("seq")
    x_at, z_at = dp // NZ, dp % NZ
    order = (
        ((x_at + jnp.arange(NX, dtype=jnp.int32))[:, None] % NX) * NZ
        + (z_at + jnp.asarray(DZ, jnp.int32))[None, :] % NZ
    ).reshape(-1)
    normed = normalize(span_store[0], norm_gain, order)
    tokens = lax.all_gather(normed, "seq", axis=0, tiled=True)

    lanes = jnp.where(jnp.arange(LANES)[:, None] == seq, target, 0)
    for bit in (1, 2, 4):
        lanes = lanes + lax.ppermute(lanes, "seq", [(s, s ^ bit) for s in range(LANES)])
    same = lanes[:, :, None] == lanes[:, None, :]
    before = jnp.arange(LANE)[None, :] < jnp.arange(LANE)[:, None]
    rank = jnp.sum((same & before[None]).astype(jnp.int32), axis=2)
    slot = (lanes * SLOTS + jnp.arange(LANES, dtype=jnp.int32)[:, None] * CAP + rank).reshape(-1)

    columns, rows = gather_weights(w_query, jnp.concatenate([key_weight, value_weight], axis=1))
    q_acc = sum(
        jnp.dot(tokens[:, at : at + w.shape[0]], w, preferred_element_type=jnp.float32) for at, w in columns
    )
    kv_acc = kv_part(tokens, rows)
    outgoing = dispatch(q_acc, kv_acc, slot)
    arrived = lax.all_to_all(
        outgoing.reshape(ND, SLOTS, -1), "dp", split_axis=0, concat_axis=0, tiled=True
    ).reshape(ND * SLOTS, -1)

    seg = segment_ids[0]
    cosine, sine = rotary_tables(seg.shape[0])
    context = attention(arrived, seg, cosine, sine)
    returned = lax.all_to_all(context, "seq", split_axis=0, concat_axis=1, tiled=True)
    return returned[None]


def solution(mesh):
    placed = (
        P("dp", "seq", None),
        P("dp", "seq"),
        P("dp", None),
        P(),
        P("dp", "seq"),
        P("dp", "seq"),
        P("dp", "seq"),
    )
    return jax.shard_map(
        shards, mesh=mesh, in_specs=placed, out_specs=P("dp", "seq", None), check_vma=False
    )
```

```python
import jax
import jax.numpy as jnp
from jax import lax
from jax.experimental import pallas as pl
from jax.experimental.pallas import tpu as pltpu
from jax.sharding import PartitionSpec as P

HEAD = 128
EPS = 1e-05
ROPE_BASE = 500000.0
NX, NZ = 4, 8
ND = NX * NZ
LANES = 8
LANE = 64
CAP = 3
SLOTS = LANES * CAP
KB = 256
BLOCK = 128
EMPTY = 2.0**100
SELF = 128
DZ = (0, 1, 7, 2, 6, 3, 5, 4)

VMEM = pl.BlockSpec(memory_space=pltpu.VMEM)
SMEM = pl.BlockSpec(memory_space=pltpu.SMEM)
ANYWHERE = pl.BlockSpec(memory_space=pl.ANY)


def from_z(value, k):
    pairs = [(x * NZ + (z + k) % NZ, x * NZ + z) for x in range(NX) for z in range(NZ)]
    return lax.ppermute(value, "dp", pairs)


def from_x(value, k):
    pairs = [(((x + k) % NX) * NZ + z, x * NZ + z) for x in range(NX) for z in range(NZ)]
    return lax.ppermute(value, "dp", pairs)


def after(values, *done):
    return lax.optimization_barrier((values, done))[0]


def normalize_kernel(x_ref, gain_ref, target_ref, out_ref):
    dp = lax.axis_index("dp")
    x_at, z_at = dp // NZ, dp % NZ
    rows = x_ref.shape[0]
    values = x_ref[...].astype(jnp.float32)
    inverse = lax.rsqrt(jnp.mean(values * values, axis=-1, keepdims=True) + EPS)
    for b in range(ND):
        dx, dz = b // NZ, DZ[b % NZ]
        start = pl.multiple_of((((x_at + dx) % NX) * NZ + (z_at + dz) % NZ) * KB, KB)
        piece = x_ref[:, pl.ds(start, KB)].astype(jnp.float32)
        gain = gain_ref[:, pl.ds(start, KB)]
        out_ref[:, b * KB : (b + 1) * KB] = (piece * inverse * gain).astype(jnp.bfloat16)
    own = lax.broadcasted_iota(jnp.int32, (rows, rows), 0) == lax.broadcasted_iota(jnp.int32, (rows, rows), 1)
    goal = jnp.sum(jnp.where(own, target_ref[...].astype(jnp.float32), 0.0), axis=1, keepdims=True)
    tail = out_ref.shape[1] - ND * KB
    out_ref[:, ND * KB :] = jnp.broadcast_to(goal, (rows, tail)).astype(jnp.bfloat16)


def normalize(stored, norm_gain, target):
    rows, width = stored.shape
    return pl.pallas_call(
        normalize_kernel,
        out_shape=jax.ShapeDtypeStruct((rows, width + HEAD), jnp.bfloat16),
        in_specs=[VMEM, VMEM, VMEM],
        out_specs=VMEM,
    )(stored, norm_gain[None, :], target)


def join_kernel(columns, *refs):
    out_ref, at = refs[-1], 0
    for ref in refs[:-1]:
        out_ref[at : at + ref.shape[0], :] = ref[:, columns:]
        at += ref.shape[0]


def join(*parts, columns=0):
    rows = sum(p.shape[0] for p in parts)
    return pl.pallas_call(
        lambda *refs: join_kernel(columns, *refs),
        out_shape=jax.ShapeDtypeStruct((rows, parts[0].shape[1] - columns), parts[0].dtype),
        in_specs=[VMEM] * len(parts),
        out_specs=VMEM,
    )(*parts)


def part_dots(tokens, pieces):
    return sum(
        jnp.dot(tokens[:, at * KB : at * KB + w.shape[0]], w, preferred_element_type=jnp.float32)
        for w, at in pieces
    )


def project(tokens, query, key_value):
    cols = query.shape[1]
    zp1, zm1 = from_z(query, 1), from_z(query, -1)
    own = jnp.concatenate([query, key_value], axis=1)
    op, om = from_x(own, 1), from_x(own, -1)
    o2 = from_x(op, 1)
    near = after(join(zp1, zm1), op, om)
    n1, n3 = from_x(near, 1), from_x(near, -1)
    zp2, zm2 = from_z(zp1, 1), from_z(zm1, -1)
    a, b = after((zp2, zm2), zp2, zm2)
    zp3, zm3 = from_z(a, 1), from_z(b, -1)
    z4 = from_z(after(zp3, zm3), 1)
    row = after(join(own, op, o2, om, columns=cols), z4)
    rp1, rm1 = from_z(row, 1), from_z(row, -1)
    n2 = from_x(after(n3, n1), -1)
    far = after(join(zp2, zm2, zp3, zm3, z4), n1, n3, row, tokens)
    f1, f3 = from_x(far, 1), from_x(far, -1)
    early = [(query, 0), (near, 1), (op[:, :cols], 8), (n1, 9), (o2[:, :cols], 16), (om[:, :cols], 24), (n3, 25)]
    q_sum = part_dots(tokens, early)
    a, b = after((rp1, rm1), rp1, rm1, n1, n3, tokens)
    rp2, rm2 = from_z(a, 1), from_z(b, -1)
    q_sum = q_sum + part_dots(tokens, [(far, 3)])
    a, b = after((rp2, rm2), rp2, rm2)
    rp3, rm3 = from_z(a, 1), from_z(b, -1)
    f1, f3 = after((f1, f3), q_sum)
    g = far.shape[0] // 2
    f2 = [from_x(f1[:g], 1), from_x(f3[g:], -1)]
    kv_sum = kv_early(tokens, [row, rp1, rm1, rp2, rm2])
    q_sum = q_sum + part_dots(tokens, [(f1, 11), (f3, 27)])
    h = row.shape[0] // 2
    a, b = after((rp3[:h], rm3[h:]), kv_sum, q_sum)
    ends = [from_z(a, 1), from_z(b, -1)]
    q_sum = q_sum + part_dots(tokens, [(n2, 17)])
    return q_sum, kv_sum, f2, [rp3, rm3, *ends]


def kv_early_kernel(tok_ref, *refs):
    out_ref = refs[-1]
    out_ref[...] = jnp.zeros_like(out_ref)

    def step(dx, carry):
        total = jnp.zeros(out_ref.shape, jnp.float32)
        rows = pl.ds(pl.multiple_of(dx * KB, KB), KB)
        for dz, ref in enumerate(refs[:-1]):
            at = pl.multiple_of((dx * NZ + dz) * KB, KB)
            total += jnp.dot(tok_ref[:, pl.ds(at, KB)], ref[rows, :], preferred_element_type=jnp.float32)
        out_ref[...] += total
        return carry

    lax.fori_loop(0, NX, step, 0)


def kv_early(tokens, blocks):
    return pl.pallas_call(
        kv_early_kernel,
        out_shape=jax.ShapeDtypeStruct((tokens.shape[0], blocks[0].shape[1]), jnp.float32),
        in_specs=[VMEM] * (1 + len(blocks)),
        out_specs=VMEM,
        compiler_params=pltpu.CompilerParams(vmem_limit_bytes=10 << 20),
    )(tokens, *blocks)


def finish_kernel(tok_ref, slot_ref, q_ref, kv_ref, f2a, f2b, rp3, rm3, ends0, ends1, out_ref, all_ref):
    tokens = tok_ref.shape[0]
    q_cols, kv_cols = q_ref.shape[1], kv_ref.shape[1]

    def dot(at, ref, low):
        return jnp.dot(
            tok_ref[:, at * KB : (at + 1) * KB], ref[low * KB : (low + 1) * KB, :], preferred_element_type=jnp.float32
        )

    kv = kv_ref[...]
    for dx in range(NX):
        end = ends0 if dx < 2 else ends1
        kv += dot(dx * NZ + 5, rp3, dx) + dot(dx * NZ + 6, rm3, dx) + dot(dx * NZ + 7, end, dx % 2)
    all_ref[:, q_cols:] = kv.astype(jnp.bfloat16)
    q, at = q_ref[...], 19 * KB
    for ref in (f2a, f2b):
        q += jnp.dot(tok_ref[:, at : at + ref.shape[0]], ref[...], preferred_element_type=jnp.float32)
        at += ref.shape[0]
    all_ref[:, :q_cols] = q.astype(jnp.bfloat16)

    def step(i, carry):
        low = pl.multiple_of(i * BLOCK, BLOCK)
        rows = low + lax.broadcasted_iota(jnp.int32, (BLOCK, tokens), 0)
        send = (rows == slot_ref[...]).astype(jnp.bfloat16)
        used = jnp.dot(send, jnp.ones((tokens, HEAD), jnp.bfloat16), preferred_element_type=jnp.float32) > 0.5
        moved = jnp.dot(send, all_ref[...], preferred_element_type=jnp.float32)
        for c in range(0, q_cols + kv_cols, HEAD):
            part = jnp.where(used, moved[:, c : c + HEAD], EMPTY)
            out_ref[pl.ds(low, BLOCK), c : c + HEAD] = part.astype(jnp.bfloat16)
        return carry

    lax.fori_loop(0, out_ref.shape[0] // BLOCK, step, 0)


def finish(tokens, slot, q_sum, kv_sum, q_late, kv_late):
    rows = tokens.shape[0]
    columns = q_sum.shape[1] + kv_sum.shape[1]
    return pl.pallas_call(
        finish_kernel,
        out_shape=jax.ShapeDtypeStruct((ND * SLOTS, columns), jnp.bfloat16),
        in_specs=[VMEM] * (4 + len(q_late) + len(kv_late)),
        out_specs=VMEM,
        scratch_shapes=[pltpu.VMEM((rows, columns), jnp.bfloat16)],
        compiler_params=pltpu.CompilerParams(vmem_limit_bytes=10 << 20),
    )(tokens, slot[None, :], q_sum, kv_sum, *q_late, *kv_late)


def attention_kernel(arr_ref, ahead_ref, segq_ref, segk_ref, cos_ref, sin_ref, out_ref, key_ref, value_ref):
    length = out_ref.shape[0]
    arrived = arr_ref.shape[0]
    valid = (arr_ref[:, :HEAD].astype(jnp.float32) < EMPTY / 2).astype(jnp.bfloat16)
    found = lax.dot_general(
        valid, ahead_ref[...], (((0,), (0,)), ((), ())), preferred_element_type=jnp.float32
    )[:1].astype(jnp.int32)
    lane = (lax.broadcasted_iota(jnp.int32, (1, arrived), 1) % SLOTS) // CAP
    place = jnp.where(found >= SELF, lane * LANE + found - SELF, -1)
    key_ref[:BLOCK, :] = jnp.zeros((BLOCK, HEAD), jnp.bfloat16)
    value_ref[:BLOCK, :] = jnp.zeros((BLOCK, HEAD), jnp.bfloat16)

    def step(b, carry):
        at = pl.multiple_of(b * BLOCK, BLOCK)
        block, window = pl.ds(at, BLOCK), pl.ds(at, 2 * BLOCK)
        new = pl.ds(pl.multiple_of(at + BLOCK, BLOCK), BLOCK)
        rows = at + lax.broadcasted_iota(jnp.int32, (BLOCK, arrived), 0)
        pick = (rows == place).astype(jnp.bfloat16)
        packed = jnp.dot(pick, arr_ref[...], preferred_element_type=jnp.float32)
        cosine, sine = cos_ref[block, :], sin_ref[block, :]

        def turn(u):
            return (u * cosine + pltpu.roll(u, HEAD // 2, 1) * sine).astype(jnp.bfloat16)

        key_ref[new, :] = turn(packed[:, 4 * HEAD : 5 * HEAD])
        value_ref[new, :] = packed[:, 5 * HEAD : 6 * HEAD].astype(jnp.bfloat16)
        keys, values = key_ref[window, :], value_ref[window, :]
        tpos = BLOCK + lax.broadcasted_iota(jnp.int32, (BLOCK, 2 * BLOCK), 0)
        upos = lax.broadcasted_iota(jnp.int32, (BLOCK, 2 * BLOCK), 1)
        allowed = (segq_ref[block, :] == segk_ref[:, window]) & (upos <= tpos)
        for h in range(4):
            q = turn(packed[:, h * HEAD : (h + 1) * HEAD])
            score = lax.dot_general(q, keys, (((1,), (1,)), ((), ())), preferred_element_type=jnp.float32)
            terms = jnp.where(allowed, jnp.exp(score * (HEAD ** -0.5)), 0.0)
            total = jnp.sum(terms, axis=-1, keepdims=True)
            weights = (terms / total).astype(jnp.bfloat16)
            context = jnp.dot(weights, values, preferred_element_type=jnp.float32)
            out_ref[block, h * HEAD : (h + 1) * HEAD] = context.astype(jnp.bfloat16)
        return carry

    lax.fori_loop(0, length // BLOCK, step, 0)


def attention(arrived, seg, cosine, sine):
    length = seg.shape[0]
    count = arrived.shape[0]
    col = jnp.arange(count, dtype=jnp.int32)
    lane = (col % SLOTS) // CAP
    ahead = ((lane[:, None] == lane[None, :]) & (col[:, None] < col[None, :])).astype(jnp.bfloat16)
    ahead = jnp.where(col[:, None] == col[None, :], float(SELF), ahead).astype(jnp.bfloat16)
    padded = jnp.concatenate([jnp.full((BLOCK,), -1, jnp.int32), seg])
    return pl.pallas_call(
        attention_kernel,
        out_shape=jax.ShapeDtypeStruct((length, 4 * HEAD), jnp.bfloat16),
        in_specs=[VMEM] * 6,
        out_specs=VMEM,
        scratch_shapes=[
            pltpu.VMEM((BLOCK + length, HEAD), jnp.bfloat16),
            pltpu.VMEM((BLOCK + length, HEAD), jnp.bfloat16),
        ],
        compiler_params=pltpu.CompilerParams(vmem_limit_bytes=10 << 20),
    )(arrived, ahead, seg[:, None], padded[None, :], cosine, sine)


def rotary_tables(length):
    half = HEAD // 2
    frequency = ROPE_BASE ** (-(jnp.arange(half, dtype=jnp.float32) * (2.0 / HEAD)))
    angles = jnp.arange(length, dtype=jnp.float32)[:, None] * frequency[None, :]
    c, s = jnp.cos(angles), jnp.sin(angles)
    return jnp.concatenate([c, c], axis=-1), jnp.concatenate([-s, s], axis=-1)


def slots_of(target):
    lanes = target.reshape(LANES, LANE)
    same = lanes[:, :, None] == lanes[:, None, :]
    before = jnp.arange(LANE)[None, :] < jnp.arange(LANE)[:, None]
    rank = jnp.sum((same & before[None]).astype(jnp.int32), axis=2)
    return (lanes * SLOTS + jnp.arange(LANES, dtype=jnp.int32)[:, None] * CAP + rank).reshape(-1)


def shards(span_store, target, segment_ids, norm_gain, w_query, key_weight, value_weight):
    normed = normalize(span_store[0], norm_gain, target)
    tokens = lax.all_gather(normed, "seq", axis=0, tiled=True)
    slot = slots_of(tokens[:, ND * KB].astype(jnp.int32))

    key_value = jnp.concatenate([key_weight, value_weight], axis=1)
    outgoing = finish(tokens, slot, *project(tokens, w_query, key_value))
    arrived = lax.all_to_all(
        outgoing.reshape(ND, SLOTS, -1), "dp", split_axis=0, concat_axis=0, tiled=True
    ).reshape(ND * SLOTS, -1)

    seg = segment_ids[0]
    cosine, sine = rotary_tables(seg.shape[0])
    context = attention(arrived, seg, cosine, sine)
    returned = lax.all_to_all(context, "seq", split_axis=0, concat_axis=1, tiled=True)
    return returned[None]


def solution(mesh):
    placed = (
        P("dp", "seq", None),
        P("dp", "seq"),
        P("dp", None),
        P(),
        P("dp", "seq"),
        P("dp", "seq"),
        P("dp", "seq"),
    )
    return jax.shard_map(
        shards, mesh=mesh, in_specs=placed, out_specs=P("dp", "seq", None), check_vma=False
    )
```

```python
import jax
import jax.numpy as jnp
from jax import lax
from jax.experimental import pallas as pl
from jax.experimental.pallas import tpu as pltpu
from jax.sharding import PartitionSpec as P

HEAD = 128
EPS = 1e-05
ROPE_BASE = 500000.0
NX, NZ = 4, 8
ND = NX * NZ
LANES = 8
LANE = 64
CAP = 3
SLOTS = LANES * CAP
KB = 256
BLOCK = 128
EMPTY = 2.0**100
SELF = 128
DZ = (0, 1, 7, 2, 6, 3, 5, 4)

VMEM = pl.BlockSpec(memory_space=pltpu.VMEM)
SMEM = pl.BlockSpec(memory_space=pltpu.SMEM)
ANYWHERE = pl.BlockSpec(memory_space=pl.ANY)


def from_z(value, k):
    pairs = [(x * NZ + (z + k) % NZ, x * NZ + z) for x in range(NX) for z in range(NZ)]
    return lax.ppermute(value, "dp", pairs)


def from_x(value, k):
    pairs = [(((x + k) % NX) * NZ + z, x * NZ + z) for x in range(NX) for z in range(NZ)]
    return lax.ppermute(value, "dp", pairs)


def after(values, *done):
    return lax.optimization_barrier((values, done))[0]


def normalize_kernel(x_ref, gain_ref, target_ref, out_ref):
    dp = lax.axis_index("dp")
    x_at, z_at = dp // NZ, dp % NZ
    rows = x_ref.shape[0]
    values = x_ref[...].astype(jnp.float32)
    inverse = lax.rsqrt(jnp.mean(values * values, axis=-1, keepdims=True) + EPS)
    for b in range(ND):
        dx, dz = b // NZ, DZ[b % NZ]
        start = pl.multiple_of((((x_at + dx) % NX) * NZ + (z_at + dz) % NZ) * KB, KB)
        piece = x_ref[:, pl.ds(start, KB)].astype(jnp.float32)
        gain = gain_ref[:, pl.ds(start, KB)]
        out_ref[:, b * KB : (b + 1) * KB] = (piece * inverse * gain).astype(jnp.bfloat16)
    own = lax.broadcasted_iota(jnp.int32, (rows, rows), 0) == lax.broadcasted_iota(jnp.int32, (rows, rows), 1)
    goal = jnp.sum(jnp.where(own, target_ref[...].astype(jnp.float32), 0.0), axis=1, keepdims=True)
    tail = out_ref.shape[1] - ND * KB
    out_ref[:, ND * KB :] = jnp.broadcast_to(goal, (rows, tail)).astype(jnp.bfloat16)


def normalize(stored, norm_gain, target):
    rows, width = stored.shape
    return pl.pallas_call(
        normalize_kernel,
        out_shape=jax.ShapeDtypeStruct((rows, width + HEAD), jnp.bfloat16),
        in_specs=[VMEM, VMEM, VMEM],
        out_specs=VMEM,
    )(stored, norm_gain[None, :], target)


def join_kernel(columns, *refs):
    out_ref, at = refs[-1], 0
    for ref in refs[:-1]:
        out_ref[at : at + ref.shape[0], :] = ref[:, columns:]
        at += ref.shape[0]


def join(*parts, columns=0):
    rows = sum(p.shape[0] for p in parts)
    return pl.pallas_call(
        lambda *refs: join_kernel(columns, *refs),
        out_shape=jax.ShapeDtypeStruct((rows, parts[0].shape[1] - columns), parts[0].dtype),
        in_specs=[VMEM] * len(parts),
        out_specs=VMEM,
    )(*parts)


def part_dots(tokens, pieces):
    return sum(
        jnp.dot(tokens[:, at * KB : at * KB + w.shape[0]], w, preferred_element_type=jnp.float32)
        for w, at in pieces
    )


def project(tokens, query, key_value):
    cols = query.shape[1]
    zp1, zm1 = from_z(query, 1), from_z(query, -1)
    own = jnp.concatenate([query, key_value], axis=1)
    op, om = from_x(own, 1), from_x(own, -1)
    o2 = from_x(op, 1)
    near = after(join(zp1, zm1), op, om)
    n1, n3 = from_x(near, 1), from_x(near, -1)
    a, b = after((zp1, zm1), op, om)
    zp2, zm2 = from_z(a, 1), from_z(b, -1)
    a, b = after((zp2, zm2), o2)
    zp3, zm3 = from_z(a, 1), from_z(b, -1)
    z4 = from_z(after(zp3, zm3, n3), 1)
    row = after(join(own, op, o2, om, columns=cols), z4, n1)
    rp1, rm1 = from_z(row, 1), from_z(row, -1)
    n2 = from_x(n3, -1)
    far = after(join(zp2, zm2, zp3, zm3, z4), n1, n3, row)
    f1, f3 = from_x(far, 1), from_x(far, -1)
    early = [(query, 0), (near, 1), (op[:, :cols], 8), (n1, 9), (o2[:, :cols], 16), (om[:, :cols], 24), (n3, 25)]
    q_sum = part_dots(tokens, early)
    a, b = after((rp1, rm1), n1, n2, tokens)
    rp2, rm2 = from_z(a, 1), from_z(b, -1)
    a, b = after((rp2, rm2), rp2, rm2)
    rp3, rm3 = from_z(a, 1), from_z(b, -1)
    f1, f3 = after((f1, f3), q_sum, rp2, rm2)
    g = far.shape[0] // 2
    f2 = [from_x(f1[:g], 1), from_x(f3[g:], -1)]
    kv_sum = kv_early(tokens, [row, rp1, rm1, rp2, rm2])
    q_sum = q_sum + part_dots(tokens, [(far, 3), (f1, 11), (f3, 27)])
    h = row.shape[0] // 2
    a, b = after((rp3[:h], rm3[h:]), kv_sum)
    ends = [from_z(a, 1), from_z(b, -1)]
    q_sum = q_sum + part_dots(tokens, [(n2, 17)])
    return q_sum, kv_sum, f2, [rp3, rm3, *ends]


def kv_early_kernel(tok_ref, *refs):
    out_ref = refs[-1]
    out_ref[...] = jnp.zeros_like(out_ref)

    def step(dx, carry):
        total = jnp.zeros(out_ref.shape, jnp.float32)
        rows = pl.ds(pl.multiple_of(dx * KB, KB), KB)
        for dz, ref in enumerate(refs[:-1]):
            at = pl.multiple_of((dx * NZ + dz) * KB, KB)
            total += jnp.dot(tok_ref[:, pl.ds(at, KB)], ref[rows, :], preferred_element_type=jnp.float32)
        out_ref[...] += total
        return carry

    lax.fori_loop(0, NX, step, 0)


def kv_early(tokens, blocks):
    return pl.pallas_call(
        kv_early_kernel,
        out_shape=jax.ShapeDtypeStruct((tokens.shape[0], blocks[0].shape[1]), jnp.float32),
        in_specs=[VMEM] * (1 + len(blocks)),
        out_specs=VMEM,
        compiler_params=pltpu.CompilerParams(vmem_limit_bytes=10 << 20),
    )(tokens, *blocks)


def finish_kernel(tok_ref, slot_ref, q_ref, kv_ref, f2a, f2b, rp3, rm3, ends0, ends1, out_ref, all_ref):
    tokens = tok_ref.shape[0]
    q_cols, kv_cols = q_ref.shape[1], kv_ref.shape[1]

    def dot(at, ref, low):
        return jnp.dot(
            tok_ref[:, at * KB : (at + 1) * KB], ref[low * KB : (low + 1) * KB, :], preferred_element_type=jnp.float32
        )

    kv = kv_ref[...]
    for dx in range(NX):
        end = ends0 if dx < 2 else ends1
        kv += dot(dx * NZ + 5, rp3, dx) + dot(dx * NZ + 6, rm3, dx) + dot(dx * NZ + 7, end, dx % 2)
    all_ref[:, q_cols:] = kv.astype(jnp.bfloat16)
    q, at = q_ref[...], 19 * KB
    for ref in (f2a, f2b):
        q += jnp.dot(tok_ref[:, at : at + ref.shape[0]], ref[...], preferred_element_type=jnp.float32)
        at += ref.shape[0]
    all_ref[:, :q_cols] = q.astype(jnp.bfloat16)

    def step(i, carry):
        low = pl.multiple_of(i * BLOCK, BLOCK)
        rows = low + lax.broadcasted_iota(jnp.int32, (BLOCK, tokens), 0)
        send = (rows == slot_ref[...]).astype(jnp.bfloat16)
        used = jnp.dot(send, jnp.ones((tokens, HEAD), jnp.bfloat16), preferred_element_type=jnp.float32) > 0.5
        moved = jnp.dot(send, all_ref[...], preferred_element_type=jnp.float32)
        for c in range(0, q_cols + kv_cols, HEAD):
            part = jnp.where(used, moved[:, c : c + HEAD], EMPTY)
            out_ref[pl.ds(low, BLOCK), c : c + HEAD] = part.astype(jnp.bfloat16)
        return carry

    lax.fori_loop(0, out_ref.shape[0] // BLOCK, step, 0)


def finish(tokens, slot, q_sum, kv_sum, q_late, kv_late):
    rows = tokens.shape[0]
    columns = q_sum.shape[1] + kv_sum.shape[1]
    return pl.pallas_call(
        finish_kernel,
        out_shape=jax.ShapeDtypeStruct((ND * SLOTS, columns), jnp.bfloat16),
        in_specs=[VMEM] * (4 + len(q_late) + len(kv_late)),
        out_specs=VMEM,
        scratch_shapes=[pltpu.VMEM((rows, columns), jnp.bfloat16)],
        compiler_params=pltpu.CompilerParams(vmem_limit_bytes=10 << 20),
    )(tokens, slot[None, :], q_sum, kv_sum, *q_late, *kv_late)


def attention_kernel(arr_ref, ahead_ref, segq_ref, segk_ref, cos_ref, sin_ref, out_ref, key_ref, value_ref):
    length = out_ref.shape[0]
    arrived = arr_ref.shape[0]
    valid = (arr_ref[:, :HEAD].astype(jnp.float32) < EMPTY / 2).astype(jnp.bfloat16)
    found = lax.dot_general(
        valid, ahead_ref[...], (((0,), (0,)), ((), ())), preferred_element_type=jnp.float32
    )[:1].astype(jnp.int32)
    lane = (lax.broadcasted_iota(jnp.int32, (1, arrived), 1) % SLOTS) // CAP
    place = jnp.where(found >= SELF, lane * LANE + found - SELF, -1)
    key_ref[:BLOCK, :] = jnp.zeros((BLOCK, HEAD), jnp.bfloat16)
    value_ref[:BLOCK, :] = jnp.zeros((BLOCK, HEAD), jnp.bfloat16)

    def step(b, carry):
        at = pl.multiple_of(b * BLOCK, BLOCK)
        block, window = pl.ds(at, BLOCK), pl.ds(at, 2 * BLOCK)
        new = pl.ds(pl.multiple_of(at + BLOCK, BLOCK), BLOCK)
        rows = at + lax.broadcasted_iota(jnp.int32, (BLOCK, arrived), 0)
        pick = (rows == place).astype(jnp.bfloat16)
        packed = jnp.dot(pick, arr_ref[...], preferred_element_type=jnp.float32)
        cosine, sine = cos_ref[block, :], sin_ref[block, :]

        def turn(u):
            return (u * cosine + pltpu.roll(u, HEAD // 2, 1) * sine).astype(jnp.bfloat16)

        key_ref[new, :] = turn(packed[:, 4 * HEAD : 5 * HEAD])
        value_ref[new, :] = packed[:, 5 * HEAD : 6 * HEAD].astype(jnp.bfloat16)
        keys, values = key_ref[window, :], value_ref[window, :]
        tpos = BLOCK + lax.broadcasted_iota(jnp.int32, (BLOCK, 2 * BLOCK), 0)
        upos = lax.broadcasted_iota(jnp.int32, (BLOCK, 2 * BLOCK), 1)
        allowed = (segq_ref[block, :] == segk_ref[:, window]) & (upos <= tpos)
        for h in range(4):
            q = turn(packed[:, h * HEAD : (h + 1) * HEAD])
            score = lax.dot_general(q, keys, (((1,), (1,)), ((), ())), preferred_element_type=jnp.float32)
            terms = jnp.where(allowed, jnp.exp(score * (HEAD ** -0.5)), 0.0)
            total = jnp.sum(terms, axis=-1, keepdims=True)
            weights = (terms / total).astype(jnp.bfloat16)
            context = jnp.dot(weights, values, preferred_element_type=jnp.float32)
            out_ref[block, h * HEAD : (h + 1) * HEAD] = context.astype(jnp.bfloat16)
        return carry

    lax.fori_loop(0, length // BLOCK, step, 0)


def attention(arrived, seg, cosine, sine):
    length = seg.shape[0]
    count = arrived.shape[0]
    col = jnp.arange(count, dtype=jnp.int32)
    lane = (col % SLOTS) // CAP
    ahead = ((lane[:, None] == lane[None, :]) & (col[:, None] < col[None, :])).astype(jnp.bfloat16)
    ahead = jnp.where(col[:, None] == col[None, :], float(SELF), ahead).astype(jnp.bfloat16)
    padded = jnp.concatenate([jnp.full((BLOCK,), -1, jnp.int32), seg])
    return pl.pallas_call(
        attention_kernel,
        out_shape=jax.ShapeDtypeStruct((length, 4 * HEAD), jnp.bfloat16),
        in_specs=[VMEM] * 6,
        out_specs=VMEM,
        scratch_shapes=[
            pltpu.VMEM((BLOCK + length, HEAD), jnp.bfloat16),
            pltpu.VMEM((BLOCK + length, HEAD), jnp.bfloat16),
        ],
        compiler_params=pltpu.CompilerParams(vmem_limit_bytes=10 << 20),
    )(arrived, ahead, seg[:, None], padded[None, :], cosine, sine)


def rotary_tables(length):
    half = HEAD // 2
    frequency = ROPE_BASE ** (-(jnp.arange(half, dtype=jnp.float32) * (2.0 / HEAD)))
    angles = jnp.arange(length, dtype=jnp.float32)[:, None] * frequency[None, :]
    c, s = jnp.cos(angles), jnp.sin(angles)
    return jnp.concatenate([c, c], axis=-1), jnp.concatenate([-s, s], axis=-1)


def slots_of(target):
    lanes = target.reshape(LANES, LANE)
    same = lanes[:, :, None] == lanes[:, None, :]
    before = jnp.arange(LANE)[None, :] < jnp.arange(LANE)[:, None]
    rank = jnp.sum((same & before[None]).astype(jnp.int32), axis=2)
    return (lanes * SLOTS + jnp.arange(LANES, dtype=jnp.int32)[:, None] * CAP + rank).reshape(-1)


def shards(span_store, target, segment_ids, norm_gain, w_query, key_weight, value_weight):
    normed = normalize(span_store[0], norm_gain, target)
    tokens = lax.all_gather(normed, "seq", axis=0, tiled=True)
    slot = slots_of(tokens[:, ND * KB].astype(jnp.int32))

    key_value = jnp.concatenate([key_weight, value_weight], axis=1)
    outgoing = finish(tokens, slot, *project(tokens, w_query, key_value))
    arrived = lax.all_to_all(
        outgoing.reshape(ND, SLOTS, -1), "dp", split_axis=0, concat_axis=0, tiled=True
    ).reshape(ND * SLOTS, -1)

    seg = segment_ids[0]
    cosine, sine = rotary_tables(seg.shape[0])
    context = attention(arrived, seg, cosine, sine)
    returned = lax.all_to_all(context, "seq", split_axis=0, concat_axis=1, tiled=True)
    return returned[None]


def solution(mesh):
    placed = (
        P("dp", "seq", None),
        P("dp", "seq"),
        P("dp", None),
        P(),
        P("dp", "seq"),
        P("dp", "seq"),
        P("dp", "seq"),
    )
    return jax.shard_map(
        shards, mesh=mesh, in_specs=placed, out_specs=P("dp", "seq", None), check_vma=False
    )
```

```python
import jax
import jax.numpy as jnp
from jax import lax
from jax.experimental import pallas as pl
from jax.experimental.pallas import tpu as pltpu
from jax.sharding import PartitionSpec as P

HEAD = 128
EPS = 1e-05
ROPE_BASE = 500000.0
NX, NZ = 4, 8
ND = NX * NZ
LANES = 8
LANE = 64
CAP = 3
SLOTS = LANES * CAP
KB = 256
BLOCK = 128
EMPTY = 2.0**100
SELF = 128
DZ = (0, 1, 7, 2, 6, 3, 5, 4)

VMEM = pl.BlockSpec(memory_space=pltpu.VMEM)
SMEM = pl.BlockSpec(memory_space=pltpu.SMEM)
ANYWHERE = pl.BlockSpec(memory_space=pl.ANY)


def from_z(value, k):
    pairs = [(x * NZ + (z + k) % NZ, x * NZ + z) for x in range(NX) for z in range(NZ)]
    return lax.ppermute(value, "dp", pairs)


def from_x(value, k):
    pairs = [(((x + k) % NX) * NZ + z, x * NZ + z) for x in range(NX) for z in range(NZ)]
    return lax.ppermute(value, "dp", pairs)


def after(values, *done):
    return lax.optimization_barrier((values, done))[0]


def normalize_kernel(x_ref, gain_ref, target_ref, out_ref):
    dp = lax.axis_index("dp")
    x_at, z_at = dp // NZ, dp % NZ
    rows = x_ref.shape[0]
    values = x_ref[...].astype(jnp.float32)
    inverse = lax.rsqrt(jnp.mean(values * values, axis=-1, keepdims=True) + EPS)
    for b in range(ND):
        dx, dz = b // NZ, DZ[b % NZ]
        start = pl.multiple_of((((x_at + dx) % NX) * NZ + (z_at + dz) % NZ) * KB, KB)
        piece = x_ref[:, pl.ds(start, KB)].astype(jnp.float32)
        gain = gain_ref[:, pl.ds(start, KB)]
        out_ref[:, b * KB : (b + 1) * KB] = (piece * inverse * gain).astype(jnp.bfloat16)
    own = lax.broadcasted_iota(jnp.int32, (rows, rows), 0) == lax.broadcasted_iota(jnp.int32, (rows, rows), 1)
    goal = jnp.sum(jnp.where(own, target_ref[...].astype(jnp.float32), 0.0), axis=1, keepdims=True)
    tail = out_ref.shape[1] - ND * KB
    out_ref[:, ND * KB :] = jnp.broadcast_to(goal, (rows, tail)).astype(jnp.bfloat16)


def normalize(stored, norm_gain, target):
    rows, width = stored.shape
    return pl.pallas_call(
        normalize_kernel,
        out_shape=jax.ShapeDtypeStruct((rows, width + HEAD), jnp.bfloat16),
        in_specs=[VMEM, VMEM, VMEM],
        out_specs=VMEM,
    )(stored, norm_gain[None, :], target)


def join_kernel(columns, *refs):
    out_ref, at = refs[-1], 0
    for ref in refs[:-1]:
        out_ref[at : at + ref.shape[0], :] = ref[:, columns:]
        at += ref.shape[0]


def join(*parts, columns=0):
    rows = sum(p.shape[0] for p in parts)
    return pl.pallas_call(
        lambda *refs: join_kernel(columns, *refs),
        out_shape=jax.ShapeDtypeStruct((rows, parts[0].shape[1] - columns), parts[0].dtype),
        in_specs=[VMEM] * len(parts),
        out_specs=VMEM,
    )(*parts)


def part_dots(tokens, pieces):
    return sum(
        jnp.dot(tokens[:, at * KB : at * KB + w.shape[0]], w, preferred_element_type=jnp.float32)
        for w, at in pieces
    )


def project(tokens, query, key_value):
    cols = query.shape[1]
    zp1, zm1 = from_z(query, 1), from_z(query, -1)
    own = jnp.concatenate([query, key_value], axis=1)
    op, om = from_x(own, 1), from_x(own, -1)
    o2 = from_x(op, 1)
    near = after(join(zp1, zm1), op, om)
    n1, n3 = from_x(near, 1), from_x(near, -1)
    a, b = after((zp1, zm1), op, om)
    zp2, zm2 = from_z(a, 1), from_z(b, -1)
    a, b = after((zp2, zm2), o2)
    zp3, zm3 = from_z(a, 1), from_z(b, -1)
    z4 = from_z(after(zp3, zm3, n3), 1)
    far = join(zp2, zm2, zp3, zm3, z4)
    row = after(join(own, op, o2, om, columns=cols), n1, far)
    rp1, rm1 = from_z(row, 1), from_z(row, -1)
    n2 = from_x(n3, -1)
    far = after(far, n1, n3)
    f1, f3 = from_x(far, 1), from_x(far, -1)
    q_sum = part_dots(tokens, [(query, 0), (near, 1), (op[:, :cols], 8), (n1, 9)])
    a, b = after((rp1, rm1), n1, n2)
    rp2, rm2 = from_z(a, 1), from_z(b, -1)
    a, b = after((rp2, rm2), q_sum)
    rp3, rm3 = from_z(a, 1), from_z(b, -1)
    q_sum = q_sum + part_dots(tokens, [(o2[:, :cols], 16), (om[:, :cols], 24), (n3, 25)])
    f1, f3 = after((f1, f3), q_sum)
    g = far.shape[0] // 2
    f2 = [from_x(f1[:g], 1), from_x(f3[g:], -1)]
    late = after(tokens, rp3, rm3)
    kv_sum = kv_early(tokens, [row, rp1, rm1, rp2, rm2])
    h = row.shape[0] // 2
    ends = [from_z(rp3[:h], 1), from_z(rm3[h:], -1)]
    q_sum = q_sum + part_dots(late, [(far, 3), (f3, 27)])
    q_sum = q_sum + part_dots(after(tokens, *ends), [(f1, 11), (n2, 17)])
    return q_sum, kv_sum, f2, [rp3, rm3, *ends]


def kv_early_kernel(tok_ref, *refs):
    out_ref = refs[-1]
    out_ref[...] = jnp.zeros_like(out_ref)

    def step(dx, carry):
        total = jnp.zeros(out_ref.shape, jnp.float32)
        rows = pl.ds(pl.multiple_of(dx * KB, KB), KB)
        for dz, ref in enumerate(refs[:-1]):
            at = pl.multiple_of((dx * NZ + dz) * KB, KB)
            total += jnp.dot(tok_ref[:, pl.ds(at, KB)], ref[rows, :], preferred_element_type=jnp.float32)
        out_ref[...] += total
        return carry

    lax.fori_loop(0, NX, step, 0)


def kv_early(tokens, blocks):
    return pl.pallas_call(
        kv_early_kernel,
        out_shape=jax.ShapeDtypeStruct((tokens.shape[0], blocks[0].shape[1]), jnp.float32),
        in_specs=[VMEM] * (1 + len(blocks)),
        out_specs=VMEM,
        compiler_params=pltpu.CompilerParams(vmem_limit_bytes=10 << 20),
    )(tokens, *blocks)


def finish_kernel(tok_ref, slot_ref, q_ref, kv_ref, f2a, f2b, rp3, rm3, ends0, ends1, out_ref, all_ref):
    tokens = tok_ref.shape[0]
    q_cols, kv_cols = q_ref.shape[1], kv_ref.shape[1]

    def dot(at, ref, low):
        return jnp.dot(
            tok_ref[:, at * KB : (at + 1) * KB], ref[low * KB : (low + 1) * KB, :], preferred_element_type=jnp.float32
        )

    kv = kv_ref[...]
    for dx in range(NX):
        end = ends0 if dx < 2 else ends1
        kv += dot(dx * NZ + 5, rp3, dx) + dot(dx * NZ + 6, rm3, dx) + dot(dx * NZ + 7, end, dx % 2)
    all_ref[:, q_cols:] = kv.astype(jnp.bfloat16)
    q, at = q_ref[...], 19 * KB
    for ref in (f2a, f2b):
        q += jnp.dot(tok_ref[:, at : at + ref.shape[0]], ref[...], preferred_element_type=jnp.float32)
        at += ref.shape[0]
    all_ref[:, :q_cols] = q.astype(jnp.bfloat16)

    def step(i, carry):
        low = pl.multiple_of(i * BLOCK, BLOCK)
        rows = low + lax.broadcasted_iota(jnp.int32, (BLOCK, tokens), 0)
        send = (rows == slot_ref[...]).astype(jnp.bfloat16)
        used = jnp.dot(send, jnp.ones((tokens, HEAD), jnp.bfloat16), preferred_element_type=jnp.float32) > 0.5
        moved = jnp.dot(send, all_ref[...], preferred_element_type=jnp.float32)
        for c in range(0, q_cols + kv_cols, HEAD):
            part = jnp.where(used, moved[:, c : c + HEAD], EMPTY)
            out_ref[pl.ds(low, BLOCK), c : c + HEAD] = part.astype(jnp.bfloat16)
        return carry

    lax.fori_loop(0, out_ref.shape[0] // BLOCK, step, 0)


def finish(tokens, slot, q_sum, kv_sum, q_late, kv_late):
    rows = tokens.shape[0]
    columns = q_sum.shape[1] + kv_sum.shape[1]
    return pl.pallas_call(
        finish_kernel,
        out_shape=jax.ShapeDtypeStruct((ND * SLOTS, columns), jnp.bfloat16),
        in_specs=[VMEM] * (4 + len(q_late) + len(kv_late)),
        out_specs=VMEM,
        scratch_shapes=[pltpu.VMEM((rows, columns), jnp.bfloat16)],
        compiler_params=pltpu.CompilerParams(vmem_limit_bytes=10 << 20),
    )(tokens, slot[None, :], q_sum, kv_sum, *q_late, *kv_late)


def attention_kernel(arr_ref, ahead_ref, segq_ref, segk_ref, cos_ref, sin_ref, out_ref, key_ref, value_ref):
    length = out_ref.shape[0]
    arrived = arr_ref.shape[0]
    valid = (arr_ref[:, :HEAD].astype(jnp.float32) < EMPTY / 2).astype(jnp.bfloat16)
    found = lax.dot_general(
        valid, ahead_ref[...], (((0,), (0,)), ((), ())), preferred_element_type=jnp.float32
    )[:1].astype(jnp.int32)
    lane = (lax.broadcasted_iota(jnp.int32, (1, arrived), 1) % SLOTS) // CAP
    place = jnp.where(found >= SELF, lane * LANE + found - SELF, -1)
    key_ref[:BLOCK, :] = jnp.zeros((BLOCK, HEAD), jnp.bfloat16)
    value_ref[:BLOCK, :] = jnp.zeros((BLOCK, HEAD), jnp.bfloat16)

    def step(b, carry):
        at = pl.multiple_of(b * BLOCK, BLOCK)
        block, window = pl.ds(at, BLOCK), pl.ds(at, 2 * BLOCK)
        new = pl.ds(pl.multiple_of(at + BLOCK, BLOCK), BLOCK)
        rows = at + lax.broadcasted_iota(jnp.int32, (BLOCK, arrived), 0)
        pick = (rows == place).astype(jnp.bfloat16)
        packed = jnp.dot(pick, arr_ref[...], preferred_element_type=jnp.float32)
        cosine, sine = cos_ref[block, :], sin_ref[block, :]

        def turn(u):
            return (u * cosine + pltpu.roll(u, HEAD // 2, 1) * sine).astype(jnp.bfloat16)

        key_ref[new, :] = turn(packed[:, 4 * HEAD : 5 * HEAD])
        value_ref[new, :] = packed[:, 5 * HEAD : 6 * HEAD].astype(jnp.bfloat16)
        keys, values = key_ref[window, :], value_ref[window, :]
        tpos = BLOCK + lax.broadcasted_iota(jnp.int32, (BLOCK, 2 * BLOCK), 0)
        upos = lax.broadcasted_iota(jnp.int32, (BLOCK, 2 * BLOCK), 1)
        allowed = (segq_ref[block, :] == segk_ref[:, window]) & (upos <= tpos)
        for h in range(4):
            q = turn(packed[:, h * HEAD : (h + 1) * HEAD])
            score = lax.dot_general(q, keys, (((1,), (1,)), ((), ())), preferred_element_type=jnp.float32)
            terms = jnp.where(allowed, jnp.exp(score * (HEAD ** -0.5)), 0.0)
            total = jnp.sum(terms, axis=-1, keepdims=True)
            weights = (terms / total).astype(jnp.bfloat16)
            context = jnp.dot(weights, values, preferred_element_type=jnp.float32)
            out_ref[block, h * HEAD : (h + 1) * HEAD] = context.astype(jnp.bfloat16)
        return carry

    lax.fori_loop(0, length // BLOCK, step, 0)


def attention(arrived, seg, cosine, sine):
    length = seg.shape[0]
    count = arrived.shape[0]
    col = jnp.arange(count, dtype=jnp.int32)
    lane = (col % SLOTS) // CAP
    ahead = ((lane[:, None] == lane[None, :]) & (col[:, None] < col[None, :])).astype(jnp.bfloat16)
    ahead = jnp.where(col[:, None] == col[None, :], float(SELF), ahead).astype(jnp.bfloat16)
    padded = jnp.concatenate([jnp.full((BLOCK,), -1, jnp.int32), seg])
    return pl.pallas_call(
        attention_kernel,
        out_shape=jax.ShapeDtypeStruct((length, 4 * HEAD), jnp.bfloat16),
        in_specs=[VMEM] * 6,
        out_specs=VMEM,
        scratch_shapes=[
            pltpu.VMEM((BLOCK + length, HEAD), jnp.bfloat16),
            pltpu.VMEM((BLOCK + length, HEAD), jnp.bfloat16),
        ],
        compiler_params=pltpu.CompilerParams(vmem_limit_bytes=10 << 20),
    )(arrived, ahead, seg[:, None], padded[None, :], cosine, sine)


def rotary_tables(length):
    half = HEAD // 2
    frequency = ROPE_BASE ** (-(jnp.arange(half, dtype=jnp.float32) * (2.0 / HEAD)))
    angles = jnp.arange(length, dtype=jnp.float32)[:, None] * frequency[None, :]
    c, s = jnp.cos(angles), jnp.sin(angles)
    return jnp.concatenate([c, c], axis=-1), jnp.concatenate([-s, s], axis=-1)


def slots_of(target):
    lanes = target.reshape(LANES, LANE)
    same = lanes[:, :, None] == lanes[:, None, :]
    before = jnp.arange(LANE)[None, :] < jnp.arange(LANE)[:, None]
    rank = jnp.sum((same & before[None]).astype(jnp.int32), axis=2)
    return (lanes * SLOTS + jnp.arange(LANES, dtype=jnp.int32)[:, None] * CAP + rank).reshape(-1)


def shards(span_store, target, segment_ids, norm_gain, w_query, key_weight, value_weight):
    normed = normalize(span_store[0], norm_gain, target)
    tokens = lax.all_gather(normed, "seq", axis=0, tiled=True)
    slot = slots_of(tokens[:, ND * KB].astype(jnp.int32))

    key_value = jnp.concatenate([key_weight, value_weight], axis=1)
    outgoing = finish(tokens, slot, *project(tokens, w_query, key_value))
    arrived = lax.all_to_all(
        outgoing.reshape(ND, SLOTS, -1), "dp", split_axis=0, concat_axis=0, tiled=True
    ).reshape(ND * SLOTS, -1)

    seg = segment_ids[0]
    cosine, sine = rotary_tables(seg.shape[0])
    context = attention(arrived, seg, cosine, sine)
    returned = lax.all_to_all(context, "seq", split_axis=0, concat_axis=1, tiled=True)
    return returned[None]


def solution(mesh):
    placed = (
        P("dp", "seq", None),
        P("dp", "seq"),
        P("dp", None),
        P(),
        P("dp", "seq"),
        P("dp", "seq"),
        P("dp", "seq"),
    )
    return jax.shard_map(
        shards, mesh=mesh, in_specs=placed, out_specs=P("dp", "seq", None), check_vma=False
    )
```

```python
import jax
import jax.numpy as jnp
from jax import lax
from jax.experimental import pallas as pl
from jax.experimental.pallas import tpu as pltpu
from jax.sharding import PartitionSpec as P

HEAD = 128
EPS = 1e-05
ROPE_BASE = 500000.0
NX, NZ = 4, 8
ND = NX * NZ
LANES = 8
LANE = 64
CAP = 3
SLOTS = LANES * CAP
KB = 256
BLOCK = 128
EMPTY = 2.0**100
SELF = 128
DZ = (0, 1, 7, 2, 6, 3, 5, 4)

VMEM = pl.BlockSpec(memory_space=pltpu.VMEM)
SMEM = pl.BlockSpec(memory_space=pltpu.SMEM)
ANYWHERE = pl.BlockSpec(memory_space=pl.ANY)


def from_z(value, k):
    pairs = [(x * NZ + (z + k) % NZ, x * NZ + z) for x in range(NX) for z in range(NZ)]
    return lax.ppermute(value, "dp", pairs)


def from_x(value, k):
    pairs = [(((x + k) % NX) * NZ + z, x * NZ + z) for x in range(NX) for z in range(NZ)]
    return lax.ppermute(value, "dp", pairs)


def after(values, *done):
    return lax.optimization_barrier((values, done))[0]


def normalize_kernel(x_ref, gain_ref, target_ref, out_ref):
    dp = lax.axis_index("dp")
    x_at, z_at = dp // NZ, dp % NZ
    rows = x_ref.shape[0]
    values = x_ref[...].astype(jnp.float32)
    inverse = lax.rsqrt(jnp.mean(values * values, axis=-1, keepdims=True) + EPS)
    for b in range(ND):
        dx, dz = b // NZ, DZ[b % NZ]
        start = pl.multiple_of((((x_at + dx) % NX) * NZ + (z_at + dz) % NZ) * KB, KB)
        piece = x_ref[:, pl.ds(start, KB)].astype(jnp.float32)
        gain = gain_ref[:, pl.ds(start, KB)]
        out_ref[:, b * KB : (b + 1) * KB] = (piece * inverse * gain).astype(jnp.bfloat16)
    own = lax.broadcasted_iota(jnp.int32, (rows, rows), 0) == lax.broadcasted_iota(jnp.int32, (rows, rows), 1)
    goal = jnp.sum(jnp.where(own, target_ref[...].astype(jnp.float32), 0.0), axis=1, keepdims=True)
    tail = out_ref.shape[1] - ND * KB
    out_ref[:, ND * KB :] = jnp.broadcast_to(goal, (rows, tail)).astype(jnp.bfloat16)


def normalize(stored, norm_gain, target):
    rows, width = stored.shape
    return pl.pallas_call(
        normalize_kernel,
        out_shape=jax.ShapeDtypeStruct((rows, width + HEAD), jnp.bfloat16),
        in_specs=[VMEM, VMEM, VMEM],
        out_specs=VMEM,
    )(stored, norm_gain[None, :], target)


def join_kernel(columns, *refs):
    out_ref, at = refs[-1], 0
    for ref in refs[:-1]:
        out_ref[at : at + ref.shape[0], :] = ref[:, columns:]
        at += ref.shape[0]


def join(*parts, columns=0):
    rows = sum(p.shape[0] for p in parts)
    return pl.pallas_call(
        lambda *refs: join_kernel(columns, *refs),
        out_shape=jax.ShapeDtypeStruct((rows, parts[0].shape[1] - columns), parts[0].dtype),
        in_specs=[VMEM] * len(parts),
        out_specs=VMEM,
    )(*parts)


def part_dots(tokens, pieces):
    return sum(
        jnp.dot(tokens[:, at * KB : at * KB + w.shape[0]], w, preferred_element_type=jnp.float32)
        for w, at in pieces
    )


def project(tokens, query, key_value):
    cols = query.shape[1]
    zp1, zm1 = from_z(query, 1), from_z(query, -1)
    own = jnp.concatenate([query, key_value], axis=1)
    op, om = from_x(own, 1), from_x(own, -1)
    o2 = from_x(op, 1)
    near = after(join(zp1, zm1), op, om)
    n1, n3 = from_x(near, 1), from_x(near, -1)
    a, b = after((zp1, zm1), op, om)
    zp2, zm2 = from_z(a, 1), from_z(b, -1)
    a, b = after((zp2, zm2), o2)
    zp3, zm3 = from_z(a, 1), from_z(b, -1)
    z4 = from_z(after(zp3, zm3, n3), 1)
    far = join(zp2, zm2, zp3, zm3, z4)
    row = after(join(own, op, o2, om, columns=cols), n1, far)
    rp1, rm1 = from_z(row, 1), from_z(row, -1)
    n2 = from_x(n3, -1)
    far = after(far, n1, n3)
    f1, f3 = from_x(far, 1), from_x(far, -1)
    q_sum = part_dots(tokens, [(query, 0), (near, 1), (op[:, :cols], 8), (n1, 9)])
    a, b = after((rp1, rm1), n1, n2)
    rp2, rm2 = from_z(a, 1), from_z(b, -1)
    a, b = after((rp2, rm2), q_sum)
    rp3, rm3 = from_z(a, 1), from_z(b, -1)
    q_sum = q_sum + part_dots(tokens, [(o2[:, :cols], 16), (om[:, :cols], 24), (n3, 25)])
    f1, f3 = after((f1, f3), q_sum)
    g = far.shape[0] // 2
    f2 = [from_x(f1[:g], 1), from_x(f3[g:], -1)]
    late = after(tokens, rp3, rm3)
    kv_sum = kv_early(tokens, [row, rp1, rm1, rp2, rm2])
    h = row.shape[0] // 2
    ends = [from_z(rp3[:h], 1), from_z(rm3[h:], -1)]
    q_sum = q_sum + part_dots(late, [(far, 3), (f3, 27)])
    q_sum = q_sum + part_dots(after(tokens, *ends), [(f1, 11), (n2, 17)])
    return q_sum, kv_sum, f2, [rp3, rm3, *ends]


def kv_early_kernel(tok_ref, *refs):
    out_ref = refs[-1]
    out_ref[...] = jnp.zeros_like(out_ref)

    def step(dx, carry):
        total = jnp.zeros(out_ref.shape, jnp.float32)
        rows = pl.ds(pl.multiple_of(dx * KB, KB), KB)
        for dz, ref in enumerate(refs[:-1]):
            at = pl.multiple_of((dx * NZ + dz) * KB, KB)
            total += jnp.dot(tok_ref[:, pl.ds(at, KB)], ref[rows, :], preferred_element_type=jnp.float32)
        out_ref[...] += total
        return carry

    lax.fori_loop(0, NX, step, 0)


def kv_early(tokens, blocks):
    return pl.pallas_call(
        kv_early_kernel,
        out_shape=jax.ShapeDtypeStruct((tokens.shape[0], blocks[0].shape[1]), jnp.float32),
        in_specs=[VMEM] * (1 + len(blocks)),
        out_specs=VMEM,
        compiler_params=pltpu.CompilerParams(vmem_limit_bytes=10 << 20),
    )(tokens, *blocks)


def finish_kernel(tok_ref, slot_ref, q_ref, kv_ref, f2a, f2b, rp3, rm3, ends0, ends1, out_ref, all_ref):
    tokens = tok_ref.shape[0]
    q_cols, kv_cols = q_ref.shape[1], kv_ref.shape[1]

    def dot(at, ref, low):
        return jnp.dot(
            tok_ref[:, at * KB : (at + 1) * KB], ref[low * KB : (low + 1) * KB, :], preferred_element_type=jnp.float32
        )

    kv = kv_ref[...]
    for dx in range(NX):
        end = ends0 if dx < 2 else ends1
        kv += dot(dx * NZ + 5, rp3, dx) + dot(dx * NZ + 6, rm3, dx) + dot(dx * NZ + 7, end, dx % 2)
    all_ref[:, q_cols:] = kv.astype(jnp.bfloat16)
    q, at = q_ref[...], 19 * KB
    for ref in (f2a, f2b):
        q += jnp.dot(tok_ref[:, at : at + ref.shape[0]], ref[...], preferred_element_type=jnp.float32)
        at += ref.shape[0]
    all_ref[:, :q_cols] = q.astype(jnp.bfloat16)

    def step(i, carry):
        low = pl.multiple_of(i * BLOCK, BLOCK)
        rows = low + lax.broadcasted_iota(jnp.int32, (BLOCK, tokens), 0)
        send = (rows == slot_ref[...]).astype(jnp.bfloat16)
        used = jnp.dot(send, jnp.ones((tokens, HEAD), jnp.bfloat16), preferred_element_type=jnp.float32) > 0.5
        moved = jnp.dot(send, all_ref[...], preferred_element_type=jnp.float32)
        for c in range(0, q_cols + kv_cols, HEAD):
            part = jnp.where(used, moved[:, c : c + HEAD], EMPTY)
            out_ref[pl.ds(low, BLOCK), c : c + HEAD] = part.astype(jnp.bfloat16)
        return carry

    lax.fori_loop(0, out_ref.shape[0] // BLOCK, step, 0, unroll=2)


def finish(tokens, slot, q_sum, kv_sum, q_late, kv_late):
    rows = tokens.shape[0]
    columns = q_sum.shape[1] + kv_sum.shape[1]
    return pl.pallas_call(
        finish_kernel,
        out_shape=jax.ShapeDtypeStruct((ND * SLOTS, columns), jnp.bfloat16),
        in_specs=[VMEM] * (4 + len(q_late) + len(kv_late)),
        out_specs=VMEM,
        scratch_shapes=[pltpu.VMEM((rows, columns), jnp.bfloat16)],
        compiler_params=pltpu.CompilerParams(vmem_limit_bytes=10 << 20),
    )(tokens, slot[None, :], q_sum, kv_sum, *q_late, *kv_late)


def attention_kernel(arr_ref, ahead_ref, segq_ref, segk_ref, cos_ref, sin_ref, out_ref, key_ref, value_ref):
    length = out_ref.shape[0]
    arrived = arr_ref.shape[0]
    valid = (arr_ref[:, :HEAD].astype(jnp.float32) < EMPTY / 2).astype(jnp.bfloat16)
    found = lax.dot_general(
        valid, ahead_ref[...], (((0,), (0,)), ((), ())), preferred_element_type=jnp.float32
    )[:1].astype(jnp.int32)
    lane = (lax.broadcasted_iota(jnp.int32, (1, arrived), 1) % SLOTS) // CAP
    place = jnp.where(found >= SELF, lane * LANE + found - SELF, -1)
    key_ref[:BLOCK, :] = jnp.zeros((BLOCK, HEAD), jnp.bfloat16)
    value_ref[:BLOCK, :] = jnp.zeros((BLOCK, HEAD), jnp.bfloat16)

    def step(b, carry):
        at = pl.multiple_of(b * BLOCK, BLOCK)
        block, window = pl.ds(at, BLOCK), pl.ds(at, 2 * BLOCK)
        new = pl.ds(pl.multiple_of(at + BLOCK, BLOCK), BLOCK)
        rows = at + lax.broadcasted_iota(jnp.int32, (BLOCK, arrived), 0)
        pick = (rows == place).astype(jnp.bfloat16)
        packed = jnp.dot(pick, arr_ref[...], preferred_element_type=jnp.float32)
        cosine, sine = cos_ref[block, :], sin_ref[block, :]

        def turn(u):
            return (u * cosine + pltpu.roll(u, HEAD // 2, 1) * sine).astype(jnp.bfloat16)

        key_ref[new, :] = turn(packed[:, 4 * HEAD : 5 * HEAD])
        value_ref[new, :] = packed[:, 5 * HEAD : 6 * HEAD].astype(jnp.bfloat16)
        keys, values = key_ref[window, :], value_ref[window, :]
        tpos = BLOCK + lax.broadcasted_iota(jnp.int32, (BLOCK, 2 * BLOCK), 0)
        upos = lax.broadcasted_iota(jnp.int32, (BLOCK, 2 * BLOCK), 1)
        allowed = (segq_ref[block, :] == segk_ref[:, window]) & (upos <= tpos)
        for h in range(4):
            q = turn(packed[:, h * HEAD : (h + 1) * HEAD])
            score = lax.dot_general(q, keys, (((1,), (1,)), ((), ())), preferred_element_type=jnp.float32)
            terms = jnp.where(allowed, jnp.exp(score * (HEAD ** -0.5)), 0.0)
            total = jnp.sum(terms, axis=-1, keepdims=True)
            weights = (terms / total).astype(jnp.bfloat16)
            context = jnp.dot(weights, values, preferred_element_type=jnp.float32)
            out_ref[block, h * HEAD : (h + 1) * HEAD] = context.astype(jnp.bfloat16)
        return carry

    lax.fori_loop(0, length // BLOCK, step, 0, unroll=2)


def attention(arrived, seg, cosine, sine):
    length = seg.shape[0]
    count = arrived.shape[0]
    col = jnp.arange(count, dtype=jnp.int32)
    lane = (col % SLOTS) // CAP
    ahead = ((lane[:, None] == lane[None, :]) & (col[:, None] < col[None, :])).astype(jnp.bfloat16)
    ahead = jnp.where(col[:, None] == col[None, :], float(SELF), ahead).astype(jnp.bfloat16)
    padded = jnp.concatenate([jnp.full((BLOCK,), -1, jnp.int32), seg])
    return pl.pallas_call(
        attention_kernel,
        out_shape=jax.ShapeDtypeStruct((length, 4 * HEAD), jnp.bfloat16),
        in_specs=[VMEM] * 6,
        out_specs=VMEM,
        scratch_shapes=[
            pltpu.VMEM((BLOCK + length, HEAD), jnp.bfloat16),
            pltpu.VMEM((BLOCK + length, HEAD), jnp.bfloat16),
        ],
        compiler_params=pltpu.CompilerParams(vmem_limit_bytes=10 << 20),
    )(arrived, ahead, seg[:, None], padded[None, :], cosine, sine)


def rotary_tables(length):
    half = HEAD // 2
    frequency = ROPE_BASE ** (-(jnp.arange(half, dtype=jnp.float32) * (2.0 / HEAD)))
    angles = jnp.arange(length, dtype=jnp.float32)[:, None] * frequency[None, :]
    c, s = jnp.cos(angles), jnp.sin(angles)
    return jnp.concatenate([c, c], axis=-1), jnp.concatenate([-s, s], axis=-1)


def slots_of(target):
    lanes = target.reshape(LANES, LANE)
    same = lanes[:, :, None] == lanes[:, None, :]
    before = jnp.arange(LANE)[None, :] < jnp.arange(LANE)[:, None]
    rank = jnp.sum((same & before[None]).astype(jnp.int32), axis=2)
    return (lanes * SLOTS + jnp.arange(LANES, dtype=jnp.int32)[:, None] * CAP + rank).reshape(-1)


def shards(span_store, target, segment_ids, norm_gain, w_query, key_weight, value_weight):
    normed = normalize(span_store[0], norm_gain, target)
    tokens = lax.all_gather(normed, "seq", axis=0, tiled=True)
    slot = slots_of(tokens[:, ND * KB].astype(jnp.int32))

    key_value = jnp.concatenate([key_weight, value_weight], axis=1)
    outgoing = finish(tokens, slot, *project(tokens, w_query, key_value))
    arrived = lax.all_to_all(
        outgoing.reshape(ND, SLOTS, -1), "dp", split_axis=0, concat_axis=0, tiled=True
    ).reshape(ND * SLOTS, -1)

    seg = segment_ids[0]
    cosine, sine = rotary_tables(seg.shape[0])
    context = attention(arrived, seg, cosine, sine)
    returned = lax.all_to_all(context, "seq", split_axis=0, concat_axis=1, tiled=True)
    return returned[None]


def solution(mesh):
    placed = (
        P("dp", "seq", None),
        P("dp", "seq"),
        P("dp", None),
        P(),
        P("dp", "seq"),
        P("dp", "seq"),
        P("dp", "seq"),
    )
    return jax.shard_map(
        shards, mesh=mesh, in_specs=placed, out_specs=P("dp", "seq", None), check_vma=False
    )
```
